32 devices in a mesh: dp: 2 (over y), seq: 16 (over z, x, core).
Axes of the slice: x: 2, y: 2, z: 4, core: 2. Of those that a mesh axis runs over, the one named last changes fastest.
Arguments:
- q_rows: bfloat16 [4096, 32, 128], P(('dp', 'seq')), parts along dimension 0
- k_rows: bfloat16 [4096, 8, 128], P(('dp', 'seq')), parts along dimension 0
- v_rows: bfloat16 [4096, 8, 128], P(('dp', 'seq')), parts along dimension 0, may hold values from -5 to 5
- doc_lengths: int32 [32], P('dp'), parts along dimension 0, may hold values from 1 to 1024, 2048 in all
- plan_dest: int32 [512], P('dp'), parts along dimension 0, may hold values from 0 to 15, as said below
- plan_slot: int32 [512], P('dp'), parts along dimension 0, may hold values from 0 to 15, as said below
Outputs:
- attn_out: bfloat16 [4096, 32, 128], P(('dp', 'seq')), parts along dimension 0
The draws below stay inside these ranges and needn't reach their ends.
There are 2 independent parts, one for each index of `dp`. The reference program is written for one: setup_inputs(seed, part) draws one part's arguments, and reference() takes and returns one part's arrays. A program takes and returns all parts, laid end to end along the dimension named above; each array names one. Nothing has to cross between parts.
Inputs may be any that keep to these rules, and one draw needn't show every extreme that they name: Loader block b is held by loader shard b // 16. plan_dest[b] is the sequence shard that block b goes to and plan_slot[b] its block position there. Every pair (plan_dest, plan_slot) occurs exactly once. One loader shard sends at most 2 blocks to one sequence shard, and exactly 2 to some. `plan_slot`: see plan_dest.
All inputs are finite; a program needn't handle non-finite values.
Results may differ from the reference program's by a relative error of at most 0.0034.
Values may be sent and summed in bfloat16 or wider, within the bound.
No kernel may reach another device: no remote copies, remote signals or barrier semaphores. Data moves between devices by JAX's collectives and lax.ppermute only.
A program may use at most 64 MiB of HBM per device.

```python
import math
import jax
import jax.numpy as jnp
import numpy as np
from jax import lax

HQ = 32
HK = 8
HD = 128
SHARDS = 16
TOKENS = 2048
MAXDOC = 1024
DOCS = 16
GROUP = 4


def key_field(key):
    base_key = jax.random.fold_in(key, 101)
    field = jax.random.truncated_normal(base_key, -4.0, 4.0, (TOKENS, HK, HD), jnp.float32)
    return field


def draw_k_rows(key, part):
    return key_field(key).astype(jnp.bfloat16)


def draw_q_rows(key, part):
    base_key = jax.random.fold_in(key, 202)
    field = jax.random.truncated_normal(base_key, -4.0, 4.0, (TOKENS, HQ, HD), jnp.float32)
    return field.astype(jnp.bfloat16)


def plan_tables(key):
    first_key = jax.random.fold_in(key, 11)
    second_key = jax.random.fold_in(key, 12)
    third_key = jax.random.fold_in(key, 13)
    fourth_key = jax.random.fold_in(key, 14)
    counter = jnp.arange(SHARDS, dtype=jnp.int32)
    offsets = jax.random.permutation(first_key, SHARDS).astype(jnp.int32)
    doubled = jax.random.randint(second_key, (SHARDS,), 0, 2).astype(jnp.int32).at[1].set(1)
    chosen = jnp.where((counter % 2 == 1) & (doubled == 1), counter - 1, counter)
    shift_of = offsets[chosen]
    order = jax.vmap(lambda sub_key: jax.random.permutation(sub_key, SHARDS))(jax.random.split(third_key, SHARDS)).astype(jnp.int32)
    dest_table = (counter[:, None] + shift_of[order]) % SHARDS
    slot_perm = jax.vmap(lambda sub_key: jax.random.permutation(sub_key, SHARDS))(jax.random.split(fourth_key, SHARDS)).astype(jnp.int32)
    slot_table = slot_perm[dest_table, order]
    return (dest_table.reshape(SHARDS * SHARDS).astype(jnp.int32), slot_table.reshape(SHARDS * SHARDS).astype(jnp.int32))


def draw_plan_dest(key, part):
    return plan_tables(key)[0]


def draw_plan_slot(key, part):
    return plan_tables(key)[1]


def levels(rng, dims, cuts, low, high):
    level, own = 1.0, jax.random.fold_in(rng, 6)
    for dim, parts in cuts:
        heights = jnp.exp(jax.random.uniform(jax.random.fold_in(own, dim), (parts,), jnp.float32, low / len(cuts), high / len(cuts)))
        level = level * jnp.repeat(heights, dims[dim] // parts).reshape([-1 if axis == dim else 1 for axis in range(len(dims))])
    return level


def split_up(number_of, total, most, slope):
    loads = [(1 << 20) // math.isqrt(rank ** slope) + 1 for rank in range(2, number_of + 1)]
    spare, given = total - most - (number_of - 1), [1] * (number_of - 1)
    while spare > 0:
        free = [i for i in range(number_of - 1) if given[i] < most]
        whole, budget = sum([loads[i] for i in free]), spare
        for i in free:
            addition = min(most - given[i], max(1, budget * loads[i] // whole), spare)
            given[i] = given[i] + addition
            spare = spare - addition
    return np.array([most] + given)


def uneven(key, count, total, limit, skew):
    if count == 2:
        one = jax.random.randint(key, (), max(1, total - limit), min(limit, total - 1) + 1)
        return jnp.stack([one, total - one])
    lengths = jnp.asarray(split_up(count, total, limit, skew), jnp.int32)
    twos = (count - 1) // 2
    source_of, receiver = lengths[1:1 + 2 * twos:2], lengths[2:2 + 2 * twos:2]
    slack = jnp.minimum(source_of - 1, limit - receiver)
    passed = jax.random.randint(jax.random.fold_in(key, 1), (twos,), 0, 1 << 20) % (slack + 1)
    lengths = lengths.at[1:1 + 2 * twos:2].set(source_of - passed).at[2:2 + 2 * twos:2].set(receiver + passed)
    return lengths[jax.random.permutation(jax.random.fold_in(key, 2), count)]


def gaussian(rng, shape, width, limit, cuts=(), kind=jnp.bfloat16):
    array = jax.random.normal(rng, shape, jnp.float32) * width
    if len(cuts) > 0:
        array = levels(rng, shape, cuts, -0.22, 0.18) * array
    return jnp.clip(array, min=-limit, max=limit).astype(kind)


def setup_inputs(seed: int = 0, part: int = 0) -> dict:
    seeds = jax.random.split(jax.random.key(seed), 7)
    own_keys = jax.random.split(jax.random.fold_in(seeds[6], part), 7)
    return {
        "q_rows": draw_q_rows(jax.random.fold_in(jax.random.fold_in(seeds[6], part), 71), part),
        "k_rows": draw_k_rows(jax.random.fold_in(jax.random.fold_in(seeds[6], part), 71), part),
        "v_rows": gaussian(own_keys[2], (TOKENS, HK, HD), 1.0, 5.0, ((0, 16),)),
        "doc_lengths": uneven(own_keys[3], DOCS, TOKENS, MAXDOC, 2).astype(jnp.int32),
        "plan_dest": draw_plan_dest(jax.random.fold_in(jax.random.fold_in(seeds[6], part), 71), part),
        "plan_slot": draw_plan_slot(jax.random.fold_in(jax.random.fold_in(seeds[6], part), 71), part),
    }


far_below = -1e30


def pack_blocks(tensor, plan_dest, plan_slot, shards):
    count = plan_dest.shape[0]
    target = (plan_dest * shards + plan_slot).astype(jnp.int32)
    inverse = jnp.zeros((count,), jnp.int32).at[target].set(jnp.arange(count, dtype=jnp.int32))
    grouped = tensor.reshape((count, tensor.shape[0] // count) + tensor.shape[1:])
    return jnp.take(grouped, inverse, axis=0).reshape(tensor.shape)


def doc_starts(doc_lengths, length_all):
    doc_ends = jnp.cumsum(doc_lengths).astype(jnp.int32)
    doc_begin = (doc_ends - doc_lengths).astype(jnp.int32)
    position = jnp.arange(length_all, dtype=jnp.int32)
    segment = jnp.sum((doc_ends[None, :] <= position[:, None]).astype(jnp.int32), axis=1)
    member = segment[:, None] == jnp.arange(doc_lengths.shape[0], dtype=jnp.int32)[None, :]
    return jnp.sum(jnp.where(member, doc_begin[None, :], 0), axis=1).astype(jnp.int32)


def attend(query_head, key_head, value_head, first_key, length_all, doc_span):
    query_block = min(512, length_all)
    key_window = min(length_all, query_block + doc_span)
    scaling = query_head.shape[-1] ** -0.5

    def one_block(number):
        query_start = (number * query_block).astype(jnp.int32)
        key_start = jnp.clip(query_start - doc_span, 0, length_all - key_window).astype(jnp.int32)
        rows_query = lax.dynamic_slice_in_dim(query_head, query_start, query_block, 0)
        rows_key = lax.dynamic_slice_in_dim(key_head, key_start, key_window, 0)
        rows_value = lax.dynamic_slice_in_dim(value_head, key_start, key_window, 0)
        scores = lax.dot_general(rows_query, rows_key, (((1,), (1,)), ((), ())), preferred_element_type=jnp.float32) * scaling
        query_pos = query_start + jnp.arange(query_block, dtype=jnp.int32)
        key_pos = key_start + jnp.arange(key_window, dtype=jnp.int32)
        first_rows = lax.dynamic_slice_in_dim(first_key, query_start, query_block, 0)
        allowed = (key_pos[None, :] <= query_pos[:, None]) & (key_pos[None, :] >= first_rows[:, None])
        scores = jnp.where(allowed, scores, far_below)
        row_max = jnp.max(scores, axis=1, keepdims=True)
        weights = jnp.exp(scores - row_max)
        total_w = jnp.sum(weights, axis=1, keepdims=True)
        mixed_rows = jnp.dot(weights.astype(jnp.bfloat16), rows_value, preferred_element_type=jnp.float32) / total_w
        return mixed_rows.astype(jnp.bfloat16)

    blocks = lax.map(one_block, jnp.arange(length_all // query_block, dtype=jnp.int32))
    return blocks.reshape(length_all, query_head.shape[-1])


def reference(q_rows, k_rows, v_rows, doc_lengths, plan_dest, plan_slot):
    query_all = pack_blocks(q_rows, plan_dest, plan_slot, SHARDS)
    keys_all = pack_blocks(k_rows, plan_dest, plan_slot, SHARDS)
    values_all = pack_blocks(v_rows, plan_dest, plan_slot, SHARDS)
    first_key = doc_starts(doc_lengths, TOKENS)

    def one_head(head_index):
        query_head = lax.dynamic_index_in_dim(query_all, head_index, 1, keepdims=False)
        key_head = lax.dynamic_index_in_dim(keys_all, head_index // GROUP, 1, keepdims=False)
        value_head = lax.dynamic_index_in_dim(values_all, head_index // GROUP, 1, keepdims=False)
        return attend(query_head, key_head, value_head, first_key, TOKENS, MAXDOC)

    result = lax.map(one_head, jnp.arange(HQ, dtype=jnp.int32))
    return jnp.transpose(result, (1, 0, 2))
```

```python
import functools

import jax
import jax.numpy as jnp
import numpy as np
from jax import lax
from jax.experimental import pallas as pl
from jax.experimental.pallas import tpu as pltpu
from jax.sharding import PartitionSpec as P

far_below = -3e38


def attend_kernel(
    lengths, dest, slot, swap, *refs, heads, shards, rows, span, tile, paired
):
    if paired:
        mine, other, out, q_packed, kv_packed, begins = refs
    else:
        mine, out, q_packed, kv_packed, begins = refs
        other = None
    length = shards * rows
    docs = lengths.shape[0]
    slots = heads + (1 if paired else 2)
    head_size = out.shape[-1]

    begins[0] = 0
    for d in range(1, docs):
        begins[d] = begins[d - 1] + lengths[d - 1]

    own = swap[0]

    def pack_shard(source, carry):
        for b in range(shards):
            block = source * shards + b
            target = dest[block] * shards + slot[block]
            base = source * (slots * shards) + b
            for h in range(heads):
                q_packed[h, target] = mine[base + h * shards]
            if paired:
                kv_packed[own, target] = mine[base + heads * shards]
                kv_packed[1 - own, target] = other[block]
            else:
                kv_packed[0, target] = mine[base + heads * shards]
                kv_packed[1, target] = mine[base + (heads + 1) * shards]
        return carry

    lax.fori_loop(0, shards, pack_shard, 0)

    q_rows = q_packed.reshape(heads, length, head_size)
    kv_rows = kv_packed.reshape(2, length, head_size)
    factor = float(head_size ** (-0.5) * np.log2(np.e))
    most = min(span // tile + 1, length // tile)

    def one_tile(number, carry):
        q_start = pl.multiple_of(number * tile, tile)
        q_end = q_start + tile

        def scan_docs(d, state):
            first, before, within = state
            begin = begins[d]
            return (
                jnp.where(begin <= q_start, begin, first),
                before + (begin <= q_start).astype(jnp.int32),
                within + (begin < q_end).astype(jnp.int32),
            )

        first, before, within = lax.fori_loop(
            0, docs, scan_docs, (jnp.int32(0), jnp.int32(0), jnp.int32(0))
        )
        q_pos = q_start + lax.broadcasted_iota(jnp.int32, (tile, 1), 0)

        def later_doc(d, firsts):
            return jnp.where(q_pos >= begins[d], begins[d], firsts)

        firsts = lax.fori_loop(before, within, later_doc, jnp.full((tile, 1), first, jnp.int32))
        count = number + 1 - lax.div(first, tile)

        for n in range(1, most + 1):

            @pl.when(count == n)
            def _(n=n):
                keys = n * tile
                k_start = pl.multiple_of(q_end - keys, tile)
                q = q_rows[:, pl.ds(q_start, tile), :].reshape(heads * tile, head_size)
                k = kv_rows[0, pl.ds(k_start, keys), :]
                v = kv_rows[1, pl.ds(k_start, keys), :]
                scores = lax.dot_general(
                    q, k, (((1,), (1,)), ((), ())), preferred_element_type=jnp.float32
                )
                k_pos = k_start + lax.broadcasted_iota(jnp.int32, (tile, keys), 1)
                allowed = (k_pos <= q_pos) & (k_pos >= firsts)
                scores = jnp.where(
                    allowed[None], scores.reshape(heads, tile, keys), far_below
                ).reshape(heads * tile, keys)
                top = jnp.max(scores, axis=1, keepdims=True)
                weights = jnp.exp2(scores * factor - top * factor)
                total = jnp.sum(weights, axis=1, keepdims=True)
                mixed = jnp.dot(
                    weights.astype(jnp.bfloat16), v, preferred_element_type=jnp.float32
                )
                mixed = (mixed * (1.0 / total)).astype(jnp.bfloat16)
                per = tile // rows
                for h in range(heads):
                    for i in range(per):
                        at = h * tile + i * rows
                        out[number * per + i, h] = mixed[at : at + rows]

        return carry

    lax.fori_loop(0, length // tile, one_tile, 0)


def attend(received, other, doc_lengths, plan_dest, plan_slot, swap, heads, span):
    shards, slots, rows, head_size = received.shape
    paired = other is not None
    per = rows // shards
    length = shards * rows
    tile = min(256, length)
    blocks = [received.reshape(shards * slots * shards, per, head_size)]
    if paired:
        blocks.append(other.reshape(shards * shards, per, head_size))
    vmem = pl.BlockSpec(memory_space=pltpu.VMEM)
    smem = pl.BlockSpec(memory_space=pltpu.SMEM)
    return pl.pallas_call(
        functools.partial(
            attend_kernel,
            heads=heads,
            shards=shards,
            rows=rows,
            span=span,
            tile=tile,
            paired=paired,
        ),
        out_shape=jax.ShapeDtypeStruct((shards, heads, rows, head_size), jnp.bfloat16),
        in_specs=[smem] * 4 + [vmem] * len(blocks),
        out_specs=vmem,
        scratch_shapes=[
            pltpu.VMEM((heads, shards * shards, per, head_size), jnp.bfloat16),
            pltpu.VMEM((2, shards * shards, per, head_size), jnp.bfloat16),
            pltpu.SMEM((doc_lengths.shape[0],), jnp.int32),
        ],
        compiler_params=pltpu.CompilerParams(vmem_limit_bytes=40 << 20),
        name="packed_attention",
    )(doc_lengths, plan_dest, plan_slot, swap, *blocks)


def per_device(q_rows, k_rows, v_rows, doc_lengths, plan_dest, plan_slot):
    shards = lax.axis_size("seq")
    my_index = lax.axis_index("seq")
    rows, heads_all, head_size = q_rows.shape
    kv_heads = k_rows.shape[1]
    span = rows * min(8, shards // 2)
    heads = heads_all // shards
    copies = shards // kv_heads
    paired = copies == 2

    q_send = q_rows.reshape(rows, shards, heads, head_size).transpose(1, 2, 0, 3)
    k_heads, v_heads = k_rows.transpose(1, 0, 2), v_rows.transpose(1, 0, 2)
    kv_send = jnp.stack([k_heads, v_heads], axis=1)
    if paired:
        kv_send = kv_send.reshape(shards, 1, rows, head_size)
    else:
        kv_send = jnp.repeat(kv_send, copies, axis=0)
    sent = jnp.concatenate([q_send, kv_send], axis=1)
    received = lax.all_to_all(sent, "seq", split_axis=0, concat_axis=0, tiled=True)
    other = None
    if paired:
        other = lax.ppermute(received[:, heads], "seq", [(i, i ^ 1) for i in range(shards)])
    swap = (my_index % 2).astype(jnp.int32).reshape(1)
    mixed = attend(received, other, doc_lengths, plan_dest, plan_slot, swap, heads, span)
    returned = lax.all_to_all(mixed, "seq", split_axis=0, concat_axis=0, tiled=True)
    return returned.reshape(heads_all, rows, head_size).transpose(1, 0, 2)


def solution(mesh):
    whole = P(("dp", "seq"), None, None)
    return jax.shard_map(
        per_device,
        mesh=mesh,
        in_specs=(whole, whole, whole, P("dp"), P("dp"), P("dp")),
        out_specs=whole,
        check_vma=False,
    )
```

```python
import functools

import jax
import jax.numpy as jnp
import numpy as np
from jax import lax
from jax.experimental import pallas as pl
from jax.experimental.pallas import tpu as pltpu
from jax.sharding import PartitionSpec as P

far_below = -3e38
vmem = pl.BlockSpec(memory_space=pltpu.VMEM)
smem = pl.BlockSpec(memory_space=pltpu.SMEM)
anywhere = pl.BlockSpec(memory_space=pl.ANY)
small = pl.CostEstimate(flops=1000, bytes_accessed=1000, transcendentals=0)


def pack_kernel(place, dest, slot, *refs, groups, heads, shards):
    units = shards // 2
    q_packed, kv_packed = refs[-2:]
    unit, core = place[0], place[1]

    def pack_block(b, carry):
        for (column, aways), blocks in zip(groups, refs):
            for i, away in enumerate(aways):
                at_chip = i * (heads + 2) * shards + b
                source = lax.bitwise_xor(unit, away) * 2 + lax.bitwise_xor(core, column)
                shard, at = dest[source * shards + b], slot[source * shards + b]
                tile = jnp.where(shard % 2 == core, shard // 2, units)
                base = tile * (heads * shards) + at
                for h in range(heads):
                    q_packed[base + h * shards] = blocks[at_chip + h * shards]
                kv_packed[0, shard * shards + at] = blocks[at_chip + heads * shards]
                kv_packed[1, shard * shards + at] = blocks[at_chip + (heads + 1) * shards]
        return carry

    lax.fori_loop(0, shards, pack_block, 0, unroll=4)


def fold(x, op):
    lanes = x[:, :128]
    for i in range(128, x.shape[1], 128):
        lanes = op(lanes, x[:, i : i + 128])
    return lanes


def attend_kernel(place, lengths, q_packed, kv_packed, *refs, away, heads, shards, rows, chunk):
    out, scores, top, total, mixed = refs[-5:]
    length = shards * rows
    head_size = q_packed.shape[-1]
    docs = lengths.shape[0]
    q_rows = q_packed.reshape(q_packed.shape[0] * q_packed.shape[1], head_size)
    kv_rows = kv_packed.reshape(2, length, head_size)
    factor = float(head_size ** (-0.5) * np.log2(np.e))
    tile = lax.bitwise_xor(place[0], away)
    q_start = (tile * 2 + place[1]) * rows
    q_end = q_start + rows

    def scan_docs(d, state):
        begin, first, before, within = state
        first = jnp.where(begin <= q_start, begin, first)
        before = before + (begin <= q_start).astype(jnp.int32)
        within = within + (begin < q_end).astype(jnp.int32)
        return begin + lengths[d], first, before, within

    zero = jnp.int32(0)
    _, first, before, within = lax.fori_loop(0, docs, scan_docs, (zero, zero, zero, zero))
    q_pos = q_start + lax.broadcasted_iota(jnp.int32, (rows, 1), 0)

    def sum_to(d, begin):
        return begin + lengths[d]

    def later_doc(d, state):
        begin, firsts = state
        return begin + lengths[d], jnp.where(q_pos >= begin, begin, firsts)

    _, firsts = lax.fori_loop(
        before,
        within,
        later_doc,
        (lax.fori_loop(0, before, sum_to, zero), jnp.full((rows, 1), first, jnp.int32)),
    )
    chunks = lax.div(q_end - first + chunk - 1, chunk)
    start = jnp.maximum(q_end - chunks * chunk, 0)
    q = q_rows[pl.ds(pl.multiple_of(tile * (heads * rows), rows), heads * rows), :]
    top[...] = jnp.full_like(top, far_below)

    def score_chunk(j, carry):
        k_start = pl.multiple_of(start + j * chunk, rows)
        k = kv_rows[0, pl.ds(k_start, chunk), :]
        s = lax.dot_general(q, k, (((1,), (1,)), ((), ())), preferred_element_type=jnp.float32)
        k_pos = k_start + lax.broadcasted_iota(jnp.int32, (rows, chunk), 1)
        allowed = (k_pos <= q_pos) & (k_pos >= firsts)
        s = jnp.where(allowed[None], s.reshape(heads, rows, chunk), far_below)
        s = s.reshape(heads * rows, chunk)
        scores[j] = s
        top[...] = jnp.maximum(top[...], fold(s, jnp.maximum))
        return carry

    lax.fori_loop(0, chunks, score_chunk, 0)
    top[...] = jnp.broadcast_to(jnp.max(top[...], axis=1, keepdims=True) * factor, top.shape)
    total[...] = jnp.zeros_like(total)
    mixed[...] = jnp.zeros_like(mixed)

    def mix_chunk(j, carry):
        v = kv_rows[1, pl.ds(pl.multiple_of(start + j * chunk, rows), chunk), :]
        shift = jnp.concatenate([top[...]] * (chunk // 128), axis=1)
        weights = jnp.exp2(scores[j] * factor - shift)
        total[...] += fold(weights, jnp.add)
        mixed[...] += jnp.dot(weights.astype(jnp.bfloat16), v, preferred_element_type=jnp.float32)
        return carry

    lax.fori_loop(0, chunks, mix_chunk, 0)
    sums = jnp.sum(total[...], axis=1, keepdims=True)
    out[...] = (mixed[...] * (1.0 / sums)).astype(jnp.bfloat16).reshape(out.shape)


def per_device(q_rows, k_rows, v_rows, doc_lengths, plan_dest, plan_slot):
    shards = lax.axis_size("seq")
    my_index = lax.axis_index("seq")
    rows, heads_all, head_size = q_rows.shape
    kv_heads = k_rows.shape[1]
    per = rows // shards
    span = rows * min(8, shards // 2)
    units = shards // 2
    unit, core = my_index // 2, my_index % 2
    heads = heads_all // units
    copies = units // kv_heads
    place = jnp.stack([unit, core]).astype(jnp.int32)

    q_send = q_rows.reshape(rows, units, heads, head_size).transpose(1, 2, 0, 3)
    kv_send = jnp.stack([k_rows, v_rows], axis=0).transpose(2, 0, 1, 3)
    kv_send = jnp.repeat(kv_send, copies, axis=0)
    sent = jnp.concatenate([q_send, kv_send], axis=1)

    def hop(x, distance):
        return lax.ppermute(x, "seq", [(i, i ^ distance) for i in range(shards)])

    def part(away):
        return lax.dynamic_index_in_dim(sent, unit ^ away, 0, keepdims=False)

    near = {away: part(away) for away in reversed(range(units))}
    for away in reversed(range(1, units)):
        near[away] = hop(near[away], 2 * away)
    half = units // 2
    far = {away: hop(near[away], 1) for away in range(units)}

    packed_shapes = (
        jax.ShapeDtypeStruct(((units + 1) * heads * shards, per, head_size), jnp.bfloat16),
        jax.ShapeDtypeStruct((2, shards * shards, per, head_size), jnp.bfloat16),
    )

    def pack(groups, arrays, packed, cost):
        blocks = [x.reshape(-1, per, head_size) for x in arrays]
        count = 3 + len(blocks)
        return pl.pallas_call(
            functools.partial(pack_kernel, groups=groups, heads=heads, shards=shards),
            out_shape=packed_shapes,
            in_specs=[smem] * 3 + [vmem] * (len(blocks) + len(packed)),
            out_specs=(vmem, vmem),
            input_output_aliases={count: 0, count + 1: 1} if packed else {},
            compiler_params=pltpu.CompilerParams(vmem_limit_bytes=24 << 20),
            cost_estimate=cost,
            name="pack_blocks",
        )(place, plan_dest, plan_slot, *blocks, *packed)

    everyone = list(range(units))
    groups = [(column, (away,)) for column in range(2) for away in everyone]
    packed = pack(groups, [x[away] for x in (near, far) for away in everyone], (), small)

    chunk = min(256, span)
    most = -(-(span + rows - 1) // chunk)
    tiles = {}
    sequence = list(reversed(range(units)))
    for turn, away in enumerate(sequence):
        after = []
        if 2 <= turn < half:
            after = [tiles[sequence[turn - 2]]]
        elif turn >= half:
            after = [tiles[sequence[half - 3 + (turn - half) * 2 // half]]]
        out = pl.pallas_call(
            functools.partial(
                attend_kernel, away=away, heads=heads, shards=shards, rows=rows, chunk=chunk
            ),
            out_shape=jax.ShapeDtypeStruct((heads, rows, head_size), jnp.bfloat16),
            in_specs=[smem] * 2 + [vmem] * 2 + [anywhere] * len(after),
            out_specs=vmem,
            scratch_shapes=[
                pltpu.VMEM((most, heads * rows, chunk), jnp.float32),
                pltpu.VMEM((heads * rows, 128), jnp.float32),
                pltpu.VMEM((heads * rows, 128), jnp.float32),
                pltpu.VMEM((heads * rows, head_size), jnp.float32),
            ],
            compiler_params=pltpu.CompilerParams(vmem_limit_bytes=24 << 20),
            cost_estimate=small,
            name="attend",
        )(place, doc_lengths, *packed, *after)
        tiles[away] = hop(out, 2 * away) if away else out
    gathered = jnp.zeros((units, heads, rows, head_size), jnp.bfloat16)
    for away in range(units):
        gathered = lax.dynamic_update_index_in_dim(gathered, tiles[away], unit ^ away, 0)
    return gathered.reshape(heads_all, rows, head_size).transpose(1, 0, 2)


def solution(mesh):
    whole = P(("dp", "seq"), None, None)
    return jax.shard_map(
        per_device,
        mesh=mesh,
        in_specs=(whole, whole, whole, P("dp"), P("dp"), P("dp")),
        out_specs=whole,
        check_vma=False,
    )
```

```python
import functools

import jax
import jax.numpy as jnp
import numpy as np
from jax import lax
from jax.experimental import pallas as pl
from jax.experimental.pallas import tpu as pltpu
from jax.sharding import PartitionSpec as P

far_below = -3e38
vmem = pl.BlockSpec(memory_space=pltpu.VMEM)
smem = pl.BlockSpec(memory_space=pltpu.SMEM)
anywhere = pl.BlockSpec(memory_space=pl.ANY)
small = pl.CostEstimate(flops=1000, bytes_accessed=1000, transcendentals=0)


def pack_kernel(place, dest, slot, *refs, groups, heads, shards):
    units = shards // 2
    q_packed, kv_packed = refs[-2:]
    unit, core = place[0], place[1]
    bases = [
        (lax.bitwise_xor(unit, away) * 2 + lax.bitwise_xor(core, column)) * shards
        for column, away in groups
    ]

    def pack_block(b, carry):
        for base, blocks in zip(bases, refs):
            shard, at = dest[base + b], slot[base + b]
            mine = lax.bitwise_and(shard, 1) == core
            tile = jnp.where(mine, lax.shift_right_logical(shard, 1), units)
            q_at, kv_at = tile * (heads * shards) + at, shard * shards + at
            for h in range(heads):
                q_packed[q_at + h * shards] = blocks[b + h * shards]
            kv_packed[0, kv_at] = blocks[b + heads * shards]
            kv_packed[1, kv_at] = blocks[b + (heads + 1) * shards]
        return carry

    lax.fori_loop(0, shards, pack_block, 0, unroll=2)


def fold(x, op):
    lanes = x[:, :128]
    for i in range(128, x.shape[1], 128):
        lanes = op(lanes, x[:, i : i + 128])
    return lanes


def attend_kernel(place, lengths, q_packed, kv_packed, *refs, aways, heads, shards, rows, chunk):
    count = len(aways)
    outs, (begins, scores, top, total, mixed) = refs[-5 - count : -5], refs[-5:]
    length = shards * rows
    head_size = q_packed.shape[-1]
    docs = lengths.shape[0]
    q_rows = q_packed.reshape(q_packed.shape[0] * q_packed.shape[1], head_size)
    kv_rows = kv_packed.reshape(2, length, head_size)
    factor = float(head_size ** (-0.5) * np.log2(np.e))

    begin = jnp.int32(0)
    for d in range(docs):
        begins[d] = begin
        begin = begin + lengths[d]

    step = aways[1] - aways[0] if count > 1 else 0

    def one_tile(turn, carry):
        away = aways[0] + turn * step
        tile = lax.bitwise_xor(place[0], away)
        q_start = (tile * 2 + place[1]) * rows
        q_end = q_start + rows
        first, before, within = jnp.int32(0), jnp.int32(0), jnp.int32(0)
        for d in range(docs):
            begin = begins[d]
            first = jnp.where(begin <= q_start, begin, first)
            before = before + (begin <= q_start).astype(jnp.int32)
            within = within + (begin < q_end).astype(jnp.int32)
        q_pos = q_start + lax.broadcasted_iota(jnp.int32, (rows, 1), 0)

        def later_doc(d, firsts):
            begin = begins[d]
            return jnp.where(q_pos >= begin, begin, firsts)

        firsts = lax.fori_loop(before, within, later_doc, jnp.full((rows, 1), first, jnp.int32))
        chunks = lax.div(q_end - first + chunk - 1, chunk)
        start = jnp.maximum(q_end - chunks * chunk, 0)
        q_at = pl.multiple_of(tile * (heads * rows), rows)

        def masked_scores(k_start, width):
            q = q_rows[pl.ds(q_at, heads * rows), :]
            k = kv_rows[0, pl.ds(k_start, width), :]
            s = lax.dot_general(q, k, (((1,), (1,)), ((), ())), preferred_element_type=jnp.float32)
            k_pos = k_start + lax.broadcasted_iota(jnp.int32, (rows, width), 1)
            allowed = (k_pos <= q_pos) & (k_pos >= firsts)
            s = jnp.where(allowed[None], s.reshape(heads, rows, width), far_below)
            return s.reshape(heads * rows, width)

        def put(value):
            for i, out in enumerate(outs):

                @pl.when(turn == i)
                def _(out=out):
                    out[...] = value.astype(jnp.bfloat16).reshape(out.shape)

        for straight in range(1, 2 + 1):

            @pl.when(chunks == straight)
            def _(width=min(straight * chunk, length)):
                k_start = pl.multiple_of(start, rows)
                s = masked_scores(k_start, width)
                peak = jnp.max(s, axis=1, keepdims=True) * factor
                weights = jnp.exp2(s * factor - peak)
                sums = jnp.sum(weights, axis=1, keepdims=True)
                v = kv_rows[1, pl.ds(k_start, width), :]
                mixed[...] = jnp.dot(
                    weights.astype(jnp.bfloat16), v, preferred_element_type=jnp.float32
                ) * (1.0 / sums)

        @pl.when(chunks > 2)
        def _():
            top[...] = jnp.full_like(top, far_below)

            def score_chunk(j, carry):
                s = masked_scores(pl.multiple_of(start + j * chunk, rows), chunk)
                scores[j] = s
                top[...] = jnp.maximum(top[...], fold(s, jnp.maximum))
                return carry

            lax.fori_loop(0, chunks, score_chunk, 0)
            top[...] = jnp.broadcast_to(jnp.max(top[...], axis=1, keepdims=True) * factor, top.shape)
            total[...] = jnp.zeros_like(total)
            mixed[...] = jnp.zeros_like(mixed)

            def mix_chunk(j, carry):
                v = kv_rows[1, pl.ds(pl.multiple_of(start + j * chunk, rows), chunk), :]
                shift = jnp.concatenate([top[...]] * (chunk // 128), axis=1)
                weights = jnp.exp2(scores[j] * factor - shift)
                total[...] += fold(weights, jnp.add)
                mixed[...] += jnp.dot(
                    weights.astype(jnp.bfloat16), v, preferred_element_type=jnp.float32
                )
                return carry

            lax.fori_loop(0, chunks, mix_chunk, 0)
            mixed[...] = mixed[...] * (1.0 / jnp.sum(total[...], axis=1, keepdims=True))

        put(mixed[...])
        return carry

    lax.fori_loop(0, count, one_tile, 0)


def per_device(q_rows, k_rows, v_rows, doc_lengths, plan_dest, plan_slot):
    shards = lax.axis_size("seq")
    my_index = lax.axis_index("seq")
    rows, heads_all, head_size = q_rows.shape
    kv_heads = k_rows.shape[1]
    per = rows // shards
    span = rows * min(8, shards // 2)
    units = shards // 2
    unit, core = my_index // 2, my_index % 2
    heads = heads_all // units
    copies = units // kv_heads
    place = jnp.stack([unit, core]).astype(jnp.int32)

    q_send = q_rows.reshape(rows, units, heads, head_size).transpose(1, 2, 0, 3)
    kv_send = jnp.stack([k_rows, v_rows], axis=0).transpose(2, 0, 1, 3)
    kv_send = jnp.repeat(kv_send, copies, axis=0)
    sent = jnp.concatenate([q_send, kv_send], axis=1)

    def hop(x, distance):
        return lax.ppermute(x, "seq", [(i, i ^ distance) for i in range(shards)])

    def part(away):
        return lax.dynamic_index_in_dim(sent, unit ^ away, 0, keepdims=False)

    near = {away: part(away) for away in reversed(range(units))}
    for away in reversed(range(1, units)):
        near[away] = hop(near[away], 2 * away)
    half = units // 2
    far = {away: hop(near[away], 1) for away in range(units)}

    packed_shapes = (
        jax.ShapeDtypeStruct(((units + 1) * heads * shards, per, head_size), jnp.bfloat16),
        jax.ShapeDtypeStruct((2, shards * shards, per, head_size), jnp.bfloat16),
    )

    def pack(groups, arrays, packed, cost):
        blocks = [x.reshape(-1, per, head_size) for x in arrays]
        count = 3 + len(blocks)
        return pl.pallas_call(
            functools.partial(pack_kernel, groups=groups, heads=heads, shards=shards),
            out_shape=packed_shapes,
            in_specs=[smem] * 3 + [vmem] * (len(blocks) + len(packed)),
            out_specs=(vmem, vmem),
            input_output_aliases={count: 0, count + 1: 1} if packed else {},
            compiler_params=pltpu.CompilerParams(vmem_limit_bytes=24 << 20),
            cost_estimate=cost,
            name="pack_blocks",
        )(place, plan_dest, plan_slot, *blocks, *packed)

    everyone = list(range(units))
    groups = [(column, away) for column in range(2) for away in everyone]
    packed = pack(groups, [x[away] for x in (near, far) for away in everyone], (), small)

    chunk = min(256, span)
    most = -(-(span + rows - 1) // chunk)
    tiles = {}

    def attend(aways, after):
        outs = pl.pallas_call(
            functools.partial(
                attend_kernel, aways=aways, heads=heads, shards=shards, rows=rows, chunk=chunk
            ),
            out_shape=[jax.ShapeDtypeStruct((heads, rows, head_size), jnp.bfloat16)] * len(aways),
            in_specs=[smem] * 2 + [vmem] * 2 + [anywhere] * len(after),
            out_specs=[vmem] * len(aways),
            scratch_shapes=[
                pltpu.SMEM((doc_lengths.shape[0],), jnp.int32),
                pltpu.VMEM((most, heads * rows, chunk), jnp.float32),
                pltpu.VMEM((heads * rows, 128), jnp.float32),
                pltpu.VMEM((heads * rows, 128), jnp.float32),
                pltpu.VMEM((heads * rows, head_size), jnp.float32),
            ],
            compiler_params=pltpu.CompilerParams(vmem_limit_bytes=24 << 20),
            cost_estimate=small,
            name="attend",
        )(place, doc_lengths, *packed, *after)
        for away, out in zip(aways, outs):
            tiles[away] = hop(out, 2 * away) if away else out

    far_tiles, near_tiles = list(reversed(range(half, units))), list(reversed(range(half)))
    attend(far_tiles[:1], [])
    attend(far_tiles[1:2], [])
    for i in range(2, half, 2):
        attend(far_tiles[i : i + 2], [])
    for i, away in enumerate(near_tiles):
        attend([away], [tiles[far_tiles[2 * i // half]]])
    gathered = jnp.zeros((units, heads, rows, head_size), jnp.bfloat16)
    for away in range(units):
        gathered = lax.dynamic_update_index_in_dim(gathered, tiles[away], unit ^ away, 0)
    return gathered.reshape(heads_all, rows, head_size).transpose(1, 0, 2)


def solution(mesh):
    whole = P(("dp", "seq"), None, None)
    return jax.shard_map(
        per_device,
        mesh=mesh,
        in_specs=(whole, whole, whole, P("dp"), P("dp"), P("dp")),
        out_specs=whole,
        check_vma=False,
    )
```

```python
import functools

import jax
import jax.numpy as jnp
import numpy as np
from jax import lax
from jax.experimental import pallas as pl
from jax.experimental.pallas import tpu as pltpu
from jax.sharding import PartitionSpec as P

far_below = -3e38
vmem = pl.BlockSpec(memory_space=pltpu.VMEM)
smem = pl.BlockSpec(memory_space=pltpu.SMEM)
anywhere = pl.BlockSpec(memory_space=pl.ANY)
small = pl.CostEstimate(flops=1000, bytes_accessed=1000, transcendentals=0)


def pack_kernel(place, dest, slot, *refs, groups, heads, shards):
    units = shards // 2
    q_packed, kv_packed = refs[-2:]
    unit, core = place[0], place[1]
    bases = [
        (lax.bitwise_xor(unit, away) * 2 + lax.bitwise_xor(core, column)) * shards
        for column, away in groups
    ]

    def pack_block(b, carry):
        for base, blocks in zip(bases, refs):
            shard, at = dest[base + b], slot[base + b]
            mine = lax.bitwise_and(shard, 1) == core
            tile = jnp.where(mine, lax.shift_right_logical(shard, 1), units)
            q_at, kv_at = tile * (heads * shards) + at, shard * shards + at
            for h in range(heads):
                q_packed[q_at + h * shards] = blocks[b + h * shards]
            kv_packed[0, kv_at] = blocks[b + heads * shards]
            kv_packed[1, kv_at] = blocks[b + (heads + 1) * shards]
        return carry

    lax.fori_loop(0, shards, pack_block, 0, unroll=2)


def fold(x, op):
    lanes = x[:, :128]
    for i in range(128, x.shape[1], 128):
        lanes = op(lanes, x[:, i : i + 128])
    return lanes


def attend_kernel(place, lengths, q_packed, kv_packed, *refs, aways, heads, shards, rows, chunk):
    count = len(aways)
    outs, (begins, scores, top, total, mixed) = refs[-5 - count : -5], refs[-5:]
    length = shards * rows
    head_size = q_packed.shape[-1]
    docs = lengths.shape[0]
    q_rows = q_packed.reshape(q_packed.shape[0] * q_packed.shape[1], head_size)
    kv_rows = kv_packed.reshape(2, length, head_size)
    factor = float(head_size ** (-0.5) * np.log2(np.e))

    begin = jnp.int32(0)
    for d in range(docs):
        begins[d] = begin
        begin = begin + lengths[d]

    step = aways[1] - aways[0] if count > 1 else 0

    def one_tile(turn, carry):
        away = aways[0] + turn * step
        tile = lax.bitwise_xor(place[0], away)
        q_start = (tile * 2 + place[1]) * rows
        q_end = q_start + rows
        first, before, within = jnp.int32(0), jnp.int32(0), jnp.int32(0)
        for d in range(docs):
            begin = begins[d]
            first = jnp.where(begin <= q_start, begin, first)
            before = before + (begin <= q_start).astype(jnp.int32)
            within = within + (begin < q_end).astype(jnp.int32)
        q_pos = q_start + lax.broadcasted_iota(jnp.int32, (rows, 1), 0)

        def later_doc(d, firsts):
            begin = begins[d]
            return jnp.where(q_pos >= begin, begin, firsts)

        firsts = lax.fori_loop(before, within, later_doc, jnp.full((rows, 1), first, jnp.int32))
        chunks = lax.div(q_end - first + chunk - 1, chunk)
        start = jnp.maximum(q_end - chunks * chunk, 0)
        q_at = pl.multiple_of(tile * (heads * rows), rows)

        def masked_scores(k_start, width):
            q = q_rows[pl.ds(q_at, heads * rows), :]
            k = kv_rows[0, pl.ds(k_start, width), :]
            s = lax.dot_general(q, k, (((1,), (1,)), ((), ())), preferred_element_type=jnp.float32)
            k_pos = k_start + lax.broadcasted_iota(jnp.int32, (rows, width), 1)
            allowed = (k_pos <= q_pos) & (k_pos >= firsts)
            s = jnp.where(allowed[None], s.reshape(heads, rows, width), far_below)
            return s.reshape(heads * rows, width)

        def put(value):
            for i, out in enumerate(outs):

                @pl.when(turn == i)
                def _(out=out):
                    out[...] = value.astype(jnp.bfloat16).reshape(out.shape)

        for straight in range(1, 2 + 1):

            @pl.when(chunks == straight)
            def _(width=min(straight * chunk, length)):
                k_start = pl.multiple_of(start, rows)
                s = masked_scores(k_start, width)
                peak = jnp.max(s, axis=1, keepdims=True) * factor
                weights = jnp.exp2(s * factor - peak)
                sums = jnp.sum(weights, axis=1, keepdims=True)
                v = kv_rows[1, pl.ds(k_start, width), :]
                mixed[...] = jnp.dot(
                    weights.astype(jnp.bfloat16), v, preferred_element_type=jnp.float32
                ) * (1.0 / sums)

        @pl.when(chunks > 2)
        def _():
            top[...] = jnp.full_like(top, far_below)

            def score_chunk(j, carry):
                s = masked_scores(pl.multiple_of(start + j * chunk, rows), chunk)
                scores[j] = s
                top[...] = jnp.maximum(top[...], fold(s, jnp.maximum))
                return carry

            lax.fori_loop(0, chunks, score_chunk, 0)
            top[...] = jnp.broadcast_to(jnp.max(top[...], axis=1, keepdims=True) * factor, top.shape)
            total[...] = jnp.zeros_like(total)
            mixed[...] = jnp.zeros_like(mixed)

            def mix_chunk(j, carry):
                v = kv_rows[1, pl.ds(pl.multiple_of(start + j * chunk, rows), chunk), :]
                shift = jnp.concatenate([top[...]] * (chunk // 128), axis=1)
                weights = jnp.exp2(scores[j] * factor - shift)
                total[...] += fold(weights, jnp.add)
                mixed[...] += jnp.dot(
                    weights.astype(jnp.bfloat16), v, preferred_element_type=jnp.float32
                )
                return carry

            lax.fori_loop(0, chunks, mix_chunk, 0)
            mixed[...] = mixed[...] * (1.0 / jnp.sum(total[...], axis=1, keepdims=True))

        put(mixed[...])
        return carry

    lax.fori_loop(0, count, one_tile, 0)


def per_device(q_rows, k_rows, v_rows, doc_lengths, plan_dest, plan_slot):
    shards = lax.axis_size("seq")
    my_index = lax.axis_index("seq")
    rows, heads_all, head_size = q_rows.shape
    kv_heads = k_rows.shape[1]
    per = rows // shards
    span = rows * min(8, shards // 2)
    units = shards // 2
    unit, core = my_index // 2, my_index % 2
    heads = heads_all // units
    copies = units // kv_heads
    place = jnp.stack([unit, core]).astype(jnp.int32)

    q_send = q_rows.reshape(rows, units, heads, head_size).transpose(1, 2, 0, 3)
    kv_send = jnp.stack([k_rows, v_rows], axis=0).transpose(2, 0, 1, 3)
    kv_send = jnp.repeat(kv_send, copies, axis=0)
    sent = jnp.concatenate([q_send, kv_send], axis=1)

    def hop(x, distance):
        return lax.ppermute(x, "seq", [(i, i ^ distance) for i in range(shards)])

    def part(away):
        return lax.dynamic_index_in_dim(sent, unit ^ away, 0, keepdims=False)

    near = {away: part(away) for away in reversed(range(units))}
    for away in reversed(range(1, units)):
        near[away] = hop(near[away], 2 * away)
    half = units // 2
    far = {away: hop(near[away], 1) for away in range(units)}

    packed_shapes = (
        jax.ShapeDtypeStruct(((units + 1) * heads * shards, per, head_size), jnp.bfloat16),
        jax.ShapeDtypeStruct((2, shards * shards, per, head_size), jnp.bfloat16),
    )

    def pack(groups, arrays, packed, cost):
        blocks = [x.reshape(-1, per, head_size) for x in arrays]
        count = 3 + len(blocks)
        return pl.pallas_call(
            functools.partial(pack_kernel, groups=groups, heads=heads, shards=shards),
            out_shape=packed_shapes,
            in_specs=[smem] * 3 + [vmem] * (len(blocks) + len(packed)),
            out_specs=(vmem, vmem),
            input_output_aliases={count: 0, count + 1: 1} if packed else {},
            compiler_params=pltpu.CompilerParams(vmem_limit_bytes=24 << 20),
            cost_estimate=cost,
            name="pack_blocks",
        )(place, plan_dest, plan_slot, *blocks, *packed)

    everyone = list(range(units))
    groups = [(column, away) for column in range(2) for away in everyone]
    packed = pack(groups, [x[away] for x in (near, far) for away in everyone], (), small)

    chunk = min(256, span)
    most = -(-(span + rows - 1) // chunk)
    tiles = {}

    def attend(aways, after):
        outs = pl.pallas_call(
            functools.partial(
                attend_kernel, aways=aways, heads=heads, shards=shards, rows=rows, chunk=chunk
            ),
            out_shape=[jax.ShapeDtypeStruct((heads, rows, head_size), jnp.bfloat16)] * len(aways),
            in_specs=[smem] * 2 + [vmem] * 2 + [anywhere] * len(after),
            out_specs=[vmem] * len(aways),
            scratch_shapes=[
                pltpu.SMEM((doc_lengths.shape[0],), jnp.int32),
                pltpu.VMEM((most, heads * rows, chunk), jnp.float32),
                pltpu.VMEM((heads * rows, 128), jnp.float32),
                pltpu.VMEM((heads * rows, 128), jnp.float32),
                pltpu.VMEM((heads * rows, head_size), jnp.float32),
            ],
            compiler_params=pltpu.CompilerParams(vmem_limit_bytes=24 << 20),
            cost_estimate=small,
            name="attend",
        )(place, doc_lengths, *packed, *after)
        for away, out in zip(aways, outs):
            tiles[away] = hop(out, 2 * away) if away else out

    far_tiles = list(reversed(range(half, units)))
    for away in far_tiles[:2] + [1]:
        attend([away], [])
    for i in range(2, half, 2):
        attend(far_tiles[i : i + 2], [tiles[1]])
    for away in range(2, half):
        attend([away], [tiles[1] if away <= half // 2 else tiles[far_tiles[0]]])
    attend([0], [tiles[far_tiles[1]]])
    gathered = jnp.zeros((units, heads, rows, head_size), jnp.bfloat16)
    for away in range(units):
        gathered = lax.dynamic_update_index_in_dim(gathered, tiles[away], unit ^ away, 0)
    return gathered.reshape(heads_all, rows, head_size).transpose(1, 0, 2)


def solution(mesh):
    whole = P(("dp", "seq"), None, None)
    return jax.shard_map(
        per_device,
        mesh=mesh,
        in_specs=(whole, whole, whole, P("dp"), P("dp"), P("dp")),
        out_specs=whole,
        check_vma=False,
    )
```

```python
import functools

import jax
import jax.numpy as jnp
import numpy as np
from jax import lax
from jax.experimental import pallas as pl
from jax.experimental.pallas import tpu as pltpu
from jax.sharding import PartitionSpec as P

far_below = -3e38
vmem = pl.BlockSpec(memory_space=pltpu.VMEM)
smem = pl.BlockSpec(memory_space=pltpu.SMEM)
anywhere = pl.BlockSpec(memory_space=pl.ANY)
small = pl.CostEstimate(flops=1000, bytes_accessed=1000, transcendentals=0)


def pack_kernel(place, dest, slot, *refs, groups, heads, shards):
    units = shards // 2
    q_packed, kv_packed = refs[-2:]
    unit, core = place[0], place[1]
    bases = [
        (lax.bitwise_xor(unit, away) * 2 + lax.bitwise_xor(core, column)) * shards
        for column, away in groups
    ]

    def pack_block(b, carry):
        for base, blocks in zip(bases, refs):
            shard, at = dest[base + b], slot[base + b]
            mine = lax.bitwise_and(shard, 1) == core
            tile = jnp.where(mine, lax.shift_right_logical(shard, 1), units)
            q_at, kv_at = tile * (heads * shards) + at, shard * shards + at
            for h in range(heads):
                q_packed[q_at + h * shards] = blocks[b + h * shards]
            kv_packed[0, kv_at] = blocks[b + heads * shards]
            kv_packed[1, kv_at] = blocks[b + (heads + 1) * shards]
        return carry

    lax.fori_loop(0, shards, pack_block, 0, unroll=2)


def fold(x, op):
    lanes = x[:, :128]
    for i in range(128, x.shape[1], 128):
        lanes = op(lanes, x[:, i : i + 128])
    return lanes


def attend_kernel(place, lengths, q_packed, kv_packed, *refs, aways, heads, shards, rows, chunk):
    count = len(aways)
    outs, (begins, scores, top, total, mixed) = refs[-5 - count : -5], refs[-5:]
    length = shards * rows
    head_size = q_packed.shape[-1]
    docs = lengths.shape[0]
    q_rows = q_packed.reshape(q_packed.shape[0] * q_packed.shape[1], head_size)
    kv_rows = kv_packed.reshape(2, length, head_size)
    factor = float(head_size ** (-0.5) * np.log2(np.e))

    begin = jnp.int32(0)
    for d in range(docs):
        begins[d] = begin
        begin = begin + lengths[d]

    def one_tile(turn, carry):
        away = aways[0]
        for i in range(1, count):
            away = jnp.where(turn == i, aways[i], away)
        tile = lax.bitwise_xor(place[0], away)
        q_start = (tile * 2 + place[1]) * rows
        q_end = q_start + rows
        first, before, within = jnp.int32(0), jnp.int32(0), jnp.int32(0)
        for d in range(docs):
            begin = begins[d]
            first = jnp.where(begin <= q_start, begin, first)
            before = before + (begin <= q_start).astype(jnp.int32)
            within = within + (begin < q_end).astype(jnp.int32)
        q_pos = q_start + lax.broadcasted_iota(jnp.int32, (rows, 1), 0)

        def later_doc(d, firsts):
            begin = begins[d]
            return jnp.where(q_pos >= begin, begin, firsts)

        firsts = lax.fori_loop(before, within, later_doc, jnp.full((rows, 1), first, jnp.int32))
        needed = q_end - first
        q_at = pl.multiple_of(tile * (heads * rows), rows)

        def masked_scores(k_start, width):
            q = q_rows[pl.ds(q_at, heads * rows), :]
            k = kv_rows[0, pl.ds(k_start, width), :]
            s = lax.dot_general(q, k, (((1,), (1,)), ((), ())), preferred_element_type=jnp.float32)
            k_pos = k_start + lax.broadcasted_iota(jnp.int32, (rows, width), 1)
            allowed = (k_pos <= q_pos) & (k_pos >= firsts)
            s = jnp.where(allowed[None], s.reshape(heads, rows, width), far_below)
            return s.reshape(heads * rows, width)

        def put(value):
            for i, out in enumerate(outs):

                @pl.when(turn == i)
                def _(out=out):
                    out[...] = value.astype(jnp.bfloat16).reshape(out.shape)

        for lower, width in ((0, chunk // 2), (chunk // 2, chunk)):

            @pl.when((needed > lower) & (needed <= width))
            def _(width=width):
                k_start = pl.multiple_of(jnp.maximum(q_end - width, 0), rows)
                s = masked_scores(k_start, width)
                peak = jnp.max(s, axis=1, keepdims=True) * factor
                weights = jnp.exp2(s * factor - peak)
                sums = jnp.sum(weights, axis=1, keepdims=True)
                v = kv_rows[1, pl.ds(k_start, width), :]
                mixed[...] = jnp.dot(
                    weights.astype(jnp.bfloat16), v, preferred_element_type=jnp.float32
                ) * (1.0 / sums)

        @pl.when(needed > chunk)
        def _():
            chunks = lax.div(needed + chunk - 1, chunk)
            start = jnp.maximum(q_end - chunks * chunk, 0)
            top[...] = jnp.full_like(top, far_below)

            def score_chunk(j, carry):
                s = masked_scores(pl.multiple_of(start + j * chunk, rows), chunk)
                scores[j] = s
                top[...] = jnp.maximum(top[...], fold(s, jnp.maximum))
                return carry

            lax.fori_loop(0, chunks, score_chunk, 0)
            top[...] = jnp.broadcast_to(jnp.max(top[...], axis=1, keepdims=True) * factor, top.shape)
            total[...] = jnp.zeros_like(total)
            mixed[...] = jnp.zeros_like(mixed)

            def mix_chunk(j, carry):
                v = kv_rows[1, pl.ds(pl.multiple_of(start + j * chunk, rows), chunk), :]
                shift = jnp.concatenate([top[...]] * (chunk // 128), axis=1)
                weights = jnp.exp2(scores[j] * factor - shift)
                total[...] += fold(weights, jnp.add)
                mixed[...] += jnp.dot(
                    weights.astype(jnp.bfloat16), v, preferred_element_type=jnp.float32
                )
                return carry

            lax.fori_loop(0, chunks, mix_chunk, 0)
            mixed[...] = mixed[...] * (1.0 / jnp.sum(total[...], axis=1, keepdims=True))

        put(mixed[...])
        return carry

    lax.fori_loop(0, count, one_tile, 0)


def per_device(q_rows, k_rows, v_rows, doc_lengths, plan_dest, plan_slot):
    shards = lax.axis_size("seq")
    my_index = lax.axis_index("seq")
    rows, heads_all, head_size = q_rows.shape
    kv_heads = k_rows.shape[1]
    per = rows // shards
    span = rows * min(8, shards // 2)
    units = shards // 2
    unit, core = my_index // 2, my_index % 2
    heads = heads_all // units
    copies = units // kv_heads
    place = jnp.stack([unit, core]).astype(jnp.int32)

    q_send = q_rows.reshape(rows, units, heads, head_size).transpose(1, 2, 0, 3)
    kv_send = jnp.stack([k_rows, v_rows], axis=0).transpose(2, 0, 1, 3)
    kv_send = jnp.repeat(kv_send, copies, axis=0)
    sent = jnp.concatenate([q_send, kv_send], axis=1)

    def hop(x, distance):
        return lax.ppermute(x, "seq", [(i, i ^ distance) for i in range(shards)])

    def part(away):
        return lax.dynamic_index_in_dim(sent, unit ^ away, 0, keepdims=False)

    near = {away: part(away) for away in reversed(range(units))}
    for away in reversed(range(1, units)):
        near[away] = hop(near[away], 2 * away)
    half = units // 2
    far = {away: hop(near[away], 1) for away in range(units)}

    packed_shapes = (
        jax.ShapeDtypeStruct(((units + 1) * heads * shards, per, head_size), jnp.bfloat16),
        jax.ShapeDtypeStruct((2, shards * shards, per, head_size), jnp.bfloat16),
    )

    def pack(groups, arrays, packed, cost):
        blocks = [x.reshape(-1, per, head_size) for x in arrays]
        count = 3 + len(blocks)
        return pl.pallas_call(
            functools.partial(pack_kernel, groups=groups, heads=heads, shards=shards),
            out_shape=packed_shapes,
            in_specs=[smem] * 3 + [vmem] * (len(blocks) + len(packed)),
            out_specs=(vmem, vmem),
            input_output_aliases={count: 0, count + 1: 1} if packed else {},
            compiler_params=pltpu.CompilerParams(vmem_limit_bytes=24 << 20),
            cost_estimate=cost,
            name="pack_blocks",
        )(place, plan_dest, plan_slot, *blocks, *packed)

    everyone = list(range(units))
    groups = [(column, away) for column in range(2) for away in everyone]
    packed = pack(groups, [x[away] for x in (near, far) for away in everyone], (), small)

    chunk = min(512, span)
    most = -(-(span + rows - 1) // chunk)
    tiles, raw = {}, {}

    def attend(aways, after):
        outs = pl.pallas_call(
            functools.partial(
                attend_kernel, aways=aways, heads=heads, shards=shards, rows=rows, chunk=chunk
            ),
            out_shape=[jax.ShapeDtypeStruct((heads, rows, head_size), jnp.bfloat16)] * len(aways),
            in_specs=[smem] * 2 + [vmem] * 2 + [anywhere] * len(after),
            out_specs=[vmem] * len(aways),
            scratch_shapes=[
                pltpu.SMEM((doc_lengths.shape[0],), jnp.int32),
                pltpu.VMEM((most, heads * rows, chunk), jnp.float32),
                pltpu.VMEM((heads * rows, 128), jnp.float32),
                pltpu.VMEM((heads * rows, 128), jnp.float32),
                pltpu.VMEM((heads * rows, head_size), jnp.float32),
            ],
            compiler_params=pltpu.CompilerParams(vmem_limit_bytes=24 << 20),
            cost_estimate=small,
            name="attend",
        )(place, doc_lengths, *packed, *after)
        for away, out in zip(aways, outs):
            raw[away] = out
            tiles[away] = hop(out, 2 * away) if away else out

    far_tiles = list(reversed(range(half, units)))
    attend((far_tiles[0], 1), [])
    attend((far_tiles[1], 2), [raw[far_tiles[0]]])
    for i in range(2, half, 2):
        attend(tuple(far_tiles[i : i + 2]), [tiles[1]])
    for away in range(3, half):
        attend((away,), [tiles[far_tiles[0]]])
    attend((0,), [tiles[far_tiles[1]]])
    gathered = jnp.zeros((units, heads, rows, head_size), jnp.bfloat16)
    for away in range(units):
        gathered = lax.dynamic_update_index_in_dim(gathered, tiles[away], unit ^ away, 0)
    return gathered.reshape(heads_all, rows, head_size).transpose(1, 0, 2)


def solution(mesh):
    whole = P(("dp", "seq"), None, None)
    return jax.shard_map(
        per_device,
        mesh=mesh,
        in_specs=(whole, whole, whole, P("dp"), P("dp"), P("dp")),
        out_specs=whole,
        check_vma=False,
    )
```

```python
import functools

import jax
import jax.numpy as jnp
import numpy as np
from jax import lax
from jax.experimental import pallas as pl
from jax.experimental.pallas import tpu as pltpu
from jax.sharding import PartitionSpec as P

far_below = -3e38
vmem = pl.BlockSpec(memory_space=pltpu.VMEM)
smem = pl.BlockSpec(memory_space=pltpu.SMEM)
anywhere = pl.BlockSpec(memory_space=pl.ANY)
small = pl.CostEstimate(flops=1000, bytes_accessed=1000, transcendentals=0)


def pack_kernel(place, targets, *refs, groups, heads, shards):
    units = shards // 2
    q_packed, kv_packed = refs[-2:]
    bits = shards.bit_length() - 1
    unit, core = place[0], place[1]
    bases = [
        (lax.bitwise_xor(unit, away) * 2 + lax.bitwise_xor(core, column)) * shards
        for column, away in groups
    ]

    def pack_block(b, carry):
        for base, blocks in zip(bases, refs):
            kv_at = targets[base + b]
            shard = lax.shift_right_logical(kv_at, bits)
            at = lax.bitwise_and(kv_at, shards - 1)
            mine = lax.bitwise_and(shard, 1) == core
            tile = jnp.where(mine, lax.shift_right_logical(shard, 1), units)
            q_at = tile * (heads * shards) + at
            for h in range(heads):
                q_packed[q_at + h * shards] = blocks[b + h * shards]
            kv_packed[0, kv_at] = blocks[b + heads * shards]
            kv_packed[1, kv_at] = blocks[b + (heads + 1) * shards]
        return carry

    lax.fori_loop(0, shards, pack_block, 0, unroll=2)


def fold(x, op):
    lanes = x[:, :128]
    for i in range(128, x.shape[1], 128):
        lanes = op(lanes, x[:, i : i + 128])
    return lanes


def attend_kernel(place, lengths, q_packed, kv_packed, *refs, aways, heads, shards, rows, chunk):
    count = len(aways)
    outs, (begins, scores, top, total, mixed) = refs[-5 - count : -5], refs[-5:]
    length = shards * rows
    head_size = q_packed.shape[-1]
    docs = lengths.shape[0]
    q_rows = q_packed.reshape(q_packed.shape[0] * q_packed.shape[1], head_size)
    kv_rows = kv_packed.reshape(2, length, head_size)
    factor = float(head_size ** (-0.5) * np.log2(np.e))

    begin = jnp.int32(0)
    for d in range(docs):
        begins[d] = begin
        begin = begin + lengths[d]

    def one_tile(turn, carry):
        away = aways[0]
        for i in range(1, count):
            away = jnp.where(turn == i, aways[i], away)
        tile = lax.bitwise_xor(place[0], away)
        q_start = (tile * 2 + place[1]) * rows
        q_end = q_start + rows
        first, before, within = jnp.int32(0), jnp.int32(0), jnp.int32(0)
        for d in range(docs):
            begin = begins[d]
            first = jnp.where(begin <= q_start, begin, first)
            before = before + (begin <= q_start).astype(jnp.int32)
            within = within + (begin < q_end).astype(jnp.int32)
        q_pos = q_start + lax.broadcasted_iota(jnp.int32, (rows, 1), 0)

        def later_doc(d, firsts):
            begin = begins[d]
            return jnp.where(q_pos >= begin, begin, firsts)

        firsts = lax.fori_loop(before, within, later_doc, jnp.full((rows, 1), first, jnp.int32))
        needed = q_end - first
        q_at = pl.multiple_of(tile * (heads * rows), rows)

        def masked_scores(k_start, width):
            q = q_rows[pl.ds(q_at, heads * rows), :]
            k = kv_rows[0, pl.ds(k_start, width), :]
            s = lax.dot_general(q, k, (((1,), (1,)), ((), ())), preferred_element_type=jnp.float32)
            k_pos = k_start + lax.broadcasted_iota(jnp.int32, (rows, width), 1)
            allowed = (k_pos <= q_pos) & (k_pos >= firsts)
            s = jnp.where(allowed[None], s.reshape(heads, rows, width), far_below)
            return s.reshape(heads * rows, width)

        def put(value):
            for i, out in enumerate(outs):

                @pl.when(turn == i)
                def _(out=out):
                    out[...] = value.astype(jnp.bfloat16).reshape(out.shape)

        for lower, width in ((0, chunk // 2), (chunk // 2, chunk)):

            @pl.when((needed > lower) & (needed <= width))
            def _(width=width):
                k_start = pl.multiple_of(jnp.maximum(q_end - width, 0), rows)
                s = masked_scores(k_start, width)
                peak = jnp.max(s, axis=1, keepdims=True) * factor
                weights = jnp.exp2(s * factor - peak)
                sums = jnp.sum(weights, axis=1, keepdims=True)
                v = kv_rows[1, pl.ds(k_start, width), :]
                mixed[...] = jnp.dot(
                    weights.astype(jnp.bfloat16), v, preferred_element_type=jnp.float32
                ) * (1.0 / sums)

        @pl.when(needed > chunk)
        def _():
            chunks = lax.div(needed + chunk - 1, chunk)
            start = jnp.maximum(q_end - chunks * chunk, 0)
            top[...] = jnp.full_like(top, far_below)

            def score_chunk(j, carry):
                s = masked_scores(pl.multiple_of(start + j * chunk, rows), chunk)
                scores[j] = s
                top[...] = jnp.maximum(top[...], fold(s, jnp.maximum))
                return carry

            lax.fori_loop(0, chunks, score_chunk, 0)
            top[...] = jnp.broadcast_to(jnp.max(top[...], axis=1, keepdims=True) * factor, top.shape)
            total[...] = jnp.zeros_like(total)
            mixed[...] = jnp.zeros_like(mixed)

            def mix_chunk(j, carry):
                v = kv_rows[1, pl.ds(pl.multiple_of(start + j * chunk, rows), chunk), :]
                shift = jnp.concatenate([top[...]] * (chunk // 128), axis=1)
                weights = jnp.exp2(scores[j] * factor - shift)
                total[...] += fold(weights, jnp.add)
                mixed[...] += jnp.dot(
                    weights.astype(jnp.bfloat16), v, preferred_element_type=jnp.float32
                )
                return carry

            lax.fori_loop(0, chunks, mix_chunk, 0)
            mixed[...] = mixed[...] * (1.0 / jnp.sum(total[...], axis=1, keepdims=True))

        put(mixed[...])
        return carry

    lax.fori_loop(0, count, one_tile, 0)


def per_device(q_rows, k_rows, v_rows, doc_lengths, plan_dest, plan_slot):
    shards = lax.axis_size("seq")
    my_index = lax.axis_index("seq")
    rows, heads_all, head_size = q_rows.shape
    kv_heads = k_rows.shape[1]
    per = rows // shards
    span = rows * min(8, shards // 2)
    units = shards // 2
    unit, core = my_index // 2, my_index % 2
    heads = heads_all // units
    copies = units // kv_heads
    place = jnp.stack([unit, core]).astype(jnp.int32)

    q_send = q_rows.reshape(rows, units, heads, head_size).transpose(1, 2, 0, 3)
    kv_send = jnp.stack([k_rows, v_rows], axis=0).transpose(2, 0, 1, 3)
    kv_send = jnp.repeat(kv_send, copies, axis=0)
    sent = jnp.concatenate([q_send, kv_send], axis=1)

    def hop(x, distance):
        return lax.ppermute(x, "seq", [(i, i ^ distance) for i in range(shards)])

    def part(away):
        return lax.dynamic_index_in_dim(sent, unit ^ away, 0, keepdims=False)

    near = {away: part(away) for away in reversed(range(units))}
    for away in reversed(range(1, units)):
        near[away] = hop(near[away], 2 * away)
    half = units // 2
    far = {away: hop(near[away], 1) for away in range(units)}

    packed_shapes = (
        jax.ShapeDtypeStruct(((units + 1) * heads * shards, per, head_size), jnp.bfloat16),
        jax.ShapeDtypeStruct((2, shards * shards, per, head_size), jnp.bfloat16),
    )

    def pack(groups, arrays, packed, cost):
        blocks = [x.reshape(-1, per, head_size) for x in arrays]
        count = 2 + len(blocks)
        return pl.pallas_call(
            functools.partial(pack_kernel, groups=groups, heads=heads, shards=shards),
            out_shape=packed_shapes,
            in_specs=[smem] * 2 + [vmem] * (len(blocks) + len(packed)),
            out_specs=(vmem, vmem),
            input_output_aliases={count: 0, count + 1: 1} if packed else {},
            compiler_params=pltpu.CompilerParams(vmem_limit_bytes=24 << 20),
            cost_estimate=cost,
            name="pack_blocks",
        )(place, plan_dest * shards + plan_slot, *blocks, *packed)

    everyone = list(range(units))
    groups = [(column, away) for column in range(2) for away in everyone]
    packed = pack(groups, [x[away] for x in (near, far) for away in everyone], (), small)

    chunk = min(512, span)
    most = -(-(span + rows - 1) // chunk)
    tiles, raw = {}, {}

    def attend(aways, after):
        outs = pl.pallas_call(
            functools.partial(
                attend_kernel, aways=aways, heads=heads, shards=shards, rows=rows, chunk=chunk
            ),
            out_shape=[jax.ShapeDtypeStruct((heads, rows, head_size), jnp.bfloat16)] * len(aways),
            in_specs=[smem] * 2 + [vmem] * 2 + [anywhere] * len(after),
            out_specs=[vmem] * len(aways),
            scratch_shapes=[
                pltpu.SMEM((doc_lengths.shape[0],), jnp.int32),
                pltpu.VMEM((most, heads * rows, chunk), jnp.float32),
                pltpu.VMEM((heads * rows, 128), jnp.float32),
                pltpu.VMEM((heads * rows, 128), jnp.float32),
                pltpu.VMEM((heads * rows, head_size), jnp.float32),
            ],
            compiler_params=pltpu.CompilerParams(vmem_limit_bytes=24 << 20),
            cost_estimate=small,
            name="attend",
        )(place, doc_lengths, *packed, *after)
        for away, out in zip(aways, outs):
            raw[away] = out
            tiles[away] = hop(out, 2 * away) if away else out

    far_tiles = [half + 1, half] + list(reversed(range(half + 2, units)))
    attend((far_tiles[0], 1), [])
    attend((far_tiles[1], 2), [raw[far_tiles[0]]])
    for i in range(2, half, 2):
        attend(tuple(far_tiles[i : i + 2]), [tiles[1]])
    for away in range(3, half):
        attend((away,), [tiles[far_tiles[0]]])
    attend((0,), [tiles[far_tiles[1]]])
    gathered = jnp.zeros((units, heads, rows, head_size), jnp.bfloat16)
    for away in range(units):
        gathered = lax.dynamic_update_index_in_dim(gathered, tiles[away], unit ^ away, 0)
    return gathered.reshape(heads_all, rows, head_size).transpose(1, 0, 2)


def solution(mesh):
    whole = P(("dp", "seq"), None, None)
    return jax.shard_map(
        per_device,
        mesh=mesh,
        in_specs=(whole, whole, whole, P("dp"), P("dp"), P("dp")),
        out_specs=whole,
        check_vma=False,
    )
```

```python
import functools

import jax
import jax.numpy as jnp
import numpy as np
from jax import lax
from jax.experimental import pallas as pl
from jax.experimental.pallas import tpu as pltpu
from jax.sharding import PartitionSpec as P

far_below = -3e38
vmem = pl.BlockSpec(memory_space=pltpu.VMEM)
smem = pl.BlockSpec(memory_space=pltpu.SMEM)
anywhere = pl.BlockSpec(memory_space=pl.ANY)
small = pl.CostEstimate(flops=1000, bytes_accessed=1000, transcendentals=0)


def pack_kernel(place, targets, *refs, groups, heads, shards):
    units = shards // 2
    q_packed, kv_packed = refs[-2:]
    bits = shards.bit_length() - 1
    unit, core = place[0], place[1]
    bases = [
        (lax.bitwise_xor(unit, away) * 2 + lax.bitwise_xor(core, column)) * shards
        for column, away in groups
    ]

    def pack_block(b, carry):
        for base, blocks in zip(bases, refs):
            kv_at = targets[base + b]
            shard = lax.shift_right_logical(kv_at, bits)
            at = lax.bitwise_and(kv_at, shards - 1)
            mine = lax.bitwise_and(shard, 1) == core
            tile = jnp.where(mine, lax.shift_right_logical(shard, 1), units)
            q_at = tile * (heads * shards) + at
            for h in range(heads):
                q_packed[q_at + h * shards] = blocks[b + h * shards]
            kv_packed[0, kv_at] = blocks[b + heads * shards]
            kv_packed[1, kv_at] = blocks[b + (heads + 1) * shards]
        return carry

    lax.fori_loop(0, shards, pack_block, 0, unroll=8)


def fold(x, op):
    lanes = x[:, :128]
    for i in range(128, x.shape[1], 128):
        lanes = op(lanes, x[:, i : i + 128])
    return lanes


def attend_kernel(place, lengths, q_packed, kv_packed, *refs, aways, heads, shards, rows, chunk):
    count = len(aways)
    outs, (begins, scores, top, total, mixed) = refs[-5 - count : -5], refs[-5:]
    length = shards * rows
    head_size = q_packed.shape[-1]
    docs = lengths.shape[0]
    q_rows = q_packed.reshape(q_packed.shape[0] * q_packed.shape[1], head_size)
    kv_rows = kv_packed.reshape(2, length, head_size)
    factor = float(head_size ** (-0.5) * np.log2(np.e))

    begin = jnp.int32(0)
    for d in range(docs):
        begins[d] = begin
        begin = begin + lengths[d]

    def one_tile(turn, carry):
        away = aways[0]
        for i in range(1, count):
            away = jnp.where(turn == i, aways[i], away)
        tile = lax.bitwise_xor(place[0], away)
        q_start = (tile * 2 + place[1]) * rows
        q_end = q_start + rows
        first, before, within = jnp.int32(0), jnp.int32(0), jnp.int32(0)
        for d in range(docs):
            begin = begins[d]
            first = jnp.where(begin <= q_start, begin, first)
            before = before + (begin <= q_start).astype(jnp.int32)
            within = within + (begin < q_end).astype(jnp.int32)
        q_pos = q_start + lax.broadcasted_iota(jnp.int32, (rows, 1), 0)

        def later_doc(d, firsts):
            begin = begins[d]
            return jnp.where(q_pos >= begin, begin, firsts)

        firsts = lax.fori_loop(before, within, later_doc, jnp.full((rows, 1), first, jnp.int32))
        needed = q_end - first
        q_at = pl.multiple_of(tile * (heads * rows), rows)

        def masked_scores(k_start, width):
            q = q_rows[pl.ds(q_at, heads * rows), :]
            k = kv_rows[0, pl.ds(k_start, width), :]
            s = lax.dot_general(q, k, (((1,), (1,)), ((), ())), preferred_element_type=jnp.float32)
            k_pos = k_start + lax.broadcasted_iota(jnp.int32, (rows, width), 1)
            allowed = (k_pos <= q_pos) & (k_pos >= firsts)
            s = jnp.where(allowed[None], s.reshape(heads, rows, width), far_below)
            return s.reshape(heads * rows, width)

        def put(value):
            for i, out in enumerate(outs):

                @pl.when(turn == i)
                def _(out=out):
                    out[...] = value.astype(jnp.bfloat16).reshape(out.shape)

        for lower, width in ((0, chunk // 2), (chunk // 2, chunk)):

            @pl.when((needed > lower) & (needed <= width))
            def _(width=width):
                k_start = pl.multiple_of(jnp.maximum(q_end - width, 0), rows)
                s = masked_scores(k_start, width)
                peak = jnp.max(s, axis=1, keepdims=True) * factor
                weights = jnp.exp2(s * factor - peak)
                sums = jnp.sum(weights, axis=1, keepdims=True)
                v = kv_rows[1, pl.ds(k_start, width), :]
                mixed[...] = jnp.dot(
                    weights.astype(jnp.bfloat16), v, preferred_element_type=jnp.float32
                ) * (1.0 / sums)

        @pl.when(needed > chunk)
        def _():
            chunks = lax.div(needed + chunk - 1, chunk)
            start = jnp.maximum(q_end - chunks * chunk, 0)
            top[...] = jnp.full_like(top, far_below)

            def score_chunk(j, carry):
                s = masked_scores(pl.multiple_of(start + j * chunk, rows), chunk)
                scores[j] = s
                top[...] = jnp.maximum(top[...], fold(s, jnp.maximum))
                return carry

            lax.fori_loop(0, chunks, score_chunk, 0)
            top[...] = jnp.broadcast_to(jnp.max(top[...], axis=1, keepdims=True) * factor, top.shape)
            total[...] = jnp.zeros_like(total)
            mixed[...] = jnp.zeros_like(mixed)

            def mix_chunk(j, carry):
                v = kv_rows[1, pl.ds(pl.multiple_of(start + j * chunk, rows), chunk), :]
                shift = jnp.concatenate([top[...]] * (chunk // 128), axis=1)
                weights = jnp.exp2(scores[j] * factor - shift)
                total[...] += fold(weights, jnp.add)
                mixed[...] += jnp.dot(
                    weights.astype(jnp.bfloat16), v, preferred_element_type=jnp.float32
                )
                return carry

            lax.fori_loop(0, chunks, mix_chunk, 0)
            mixed[...] = mixed[...] * (1.0 / jnp.sum(total[...], axis=1, keepdims=True))

        put(mixed[...])
        return carry

    lax.fori_loop(0, count, one_tile, 0)


def per_device(q_rows, k_rows, v_rows, doc_lengths, plan_dest, plan_slot):
    shards = lax.axis_size("seq")
    my_index = lax.axis_index("seq")
    rows, heads_all, head_size = q_rows.shape
    kv_heads = k_rows.shape[1]
    per = rows // shards
    span = rows * min(8, shards // 2)
    units = shards // 2
    unit, core = my_index // 2, my_index % 2
    heads = heads_all // units
    copies = units // kv_heads
    place = jnp.stack([unit, core]).astype(jnp.int32)

    q_send = q_rows.reshape(rows, units, heads, head_size).transpose(1, 2, 0, 3)
    kv_send = jnp.stack([k_rows, v_rows], axis=0).transpose(2, 0, 1, 3)
    kv_send = jnp.repeat(kv_send, copies, axis=0)
    sent = jnp.concatenate([q_send, kv_send], axis=1)

    def hop(x, distance):
        return lax.ppermute(x, "seq", [(i, i ^ distance) for i in range(shards)])

    def part(away):
        return lax.dynamic_index_in_dim(sent, unit ^ away, 0, keepdims=False)

    near = {away: part(away) for away in reversed(range(units))}
    for away in reversed(range(1, units)):
        near[away] = hop(near[away], 2 * away)
    half = units // 2
    far = {away: hop(near[away], 1) for away in range(units)}

    packed_shapes = (
        jax.ShapeDtypeStruct(((units + 1) * heads * shards, per, head_size), jnp.bfloat16),
        jax.ShapeDtypeStruct((2, shards * shards, per, head_size), jnp.bfloat16),
    )

    def pack(groups, arrays, packed, cost):
        blocks = [x.reshape(-1, per, head_size) for x in arrays]
        count = 2 + len(blocks)
        return pl.pallas_call(
            functools.partial(pack_kernel, groups=groups, heads=heads, shards=shards),
            out_shape=packed_shapes,
            in_specs=[smem] * 2 + [vmem] * (len(blocks) + len(packed)),
            out_specs=(vmem, vmem),
            input_output_aliases={count: 0, count + 1: 1} if packed else {},
            compiler_params=pltpu.CompilerParams(vmem_limit_bytes=24 << 20),
            cost_estimate=cost,
            name="pack_blocks",
        )(place, plan_dest * shards + plan_slot, *blocks, *packed)

    everyone = list(range(units))
    groups = [(column, away) for column in range(2) for away in everyone]
    packed = pack(groups, [x[away] for x in (near, far) for away in everyone], (), small)

    chunk = min(512, span)
    most = -(-(span + rows - 1) // chunk)
    tiles, raw = {}, {}

    def attend(aways, after):
        outs = pl.pallas_call(
            functools.partial(
                attend_kernel, aways=aways, heads=heads, shards=shards, rows=rows, chunk=chunk
            ),
            out_shape=[jax.ShapeDtypeStruct((heads, rows, head_size), jnp.bfloat16)] * len(aways),
            in_specs=[smem] * 2 + [vmem] * 2 + [anywhere] * len(after),
            out_specs=[vmem] * len(aways),
            scratch_shapes=[
                pltpu.SMEM((doc_lengths.shape[0],), jnp.int32),
                pltpu.VMEM((most, heads * rows, chunk), jnp.float32),
                pltpu.VMEM((heads * rows, 128), jnp.float32),
                pltpu.VMEM((heads * rows, 128), jnp.float32),
                pltpu.VMEM((heads * rows, head_size), jnp.float32),
            ],
            compiler_params=pltpu.CompilerParams(vmem_limit_bytes=24 << 20),
            cost_estimate=small,
            name="attend",
        )(place, doc_lengths, *packed, *after)
        for away, out in zip(aways, outs):
            raw[away] = out
            tiles[away] = hop(out, 2 * away) if away else out

    far_tiles = [half + 1, half] + list(reversed(range(half + 2, units)))
    attend((far_tiles[0], 1), [])
    attend((far_tiles[1], 2), [raw[far_tiles[0]]])
    for i in range(2, half, 2):
        attend(tuple(far_tiles[i : i + 2]), [tiles[1]])
    for away in range(3, half):
        attend((away,), [tiles[far_tiles[0]]])
    attend((0,), [tiles[far_tiles[1]]])
    gathered = jnp.zeros((units, heads, rows, head_size), jnp.bfloat16)
    for away in range(units):
        gathered = lax.dynamic_update_index_in_dim(gathered, tiles[away], unit ^ away, 0)
    return gathered.reshape(heads_all, rows, head_size).transpose(1, 0, 2)


def solution(mesh):
    whole = P(("dp", "seq"), None, None)
    return jax.shard_map(
        per_device,
        mesh=mesh,
        in_specs=(whole, whole, whole, P("dp"), P("dp"), P("dp")),
        out_specs=whole,
        check_vma=False,
    )
```

```python
import functools

import jax
import jax.numpy as jnp
import numpy as np
from jax import lax
from jax.experimental import pallas as pl
from jax.experimental.pallas import tpu as pltpu
from jax.sharding import PartitionSpec as P

far_below = -3e38
vmem = pl.BlockSpec(memory_space=pltpu.VMEM)
smem = pl.BlockSpec(memory_space=pltpu.SMEM)
anywhere = pl.BlockSpec(memory_space=pl.ANY)
small = pl.CostEstimate(flops=1000, bytes_accessed=1000, transcendentals=0)


def pack_kernel(place, targets, *refs, groups, heads, shards):
    units = shards // 2
    q_packed, kv_packed = refs[-2:]
    bits = shards.bit_length() - 1
    unit, core = place[0], place[1]
    bases = [
        (lax.bitwise_xor(unit, away) * 2 + lax.bitwise_xor(core, column)) * shards
        for column, away in groups
    ]

    def pack_block(b, carry):
        for base, blocks in zip(bases, refs):
            kv_at = targets[base + b]
            shard = lax.shift_right_logical(kv_at, bits)
            at = lax.bitwise_and(kv_at, shards - 1)
            mine = lax.bitwise_and(shard, 1) == core
            tile = jnp.where(mine, lax.shift_right_logical(shard, 1), units)
            q_at = tile * (heads * shards) + at
            for h in range(heads):
                q_packed[q_at + h * shards] = blocks[b + h * shards]
            kv_packed[0, kv_at] = blocks[b + heads * shards]
            kv_packed[1, kv_at] = blocks[b + (heads + 1) * shards]
        return carry

    lax.fori_loop(0, shards, pack_block, 0, unroll=2)


def fold(x, op):
    lanes = x[:, :128]
    for i in range(128, x.shape[1], 128):
        lanes = op(lanes, x[:, i : i + 128])
    return lanes


def attend_kernel(place, lengths, q_packed, kv_packed, *refs, aways, heads, shards, rows, chunk):
    count = len(aways)
    outs, (begins, scores, top, total, mixed) = refs[-5 - count : -5], refs[-5:]
    length = shards * rows
    head_size = q_packed.shape[-1]
    docs = lengths.shape[0]
    q_rows = q_packed.reshape(q_packed.shape[0] * q_packed.shape[1], head_size)
    kv_rows = kv_packed.reshape(2, length, head_size)
    factor = float(head_size ** (-0.5) * np.log2(np.e))

    begin = jnp.int32(0)
    for d in range(docs):
        begins[d] = begin
        begin = begin + lengths[d]

    def one_tile(turn, carry):
        away = aways[0]
        for i in range(1, count):
            away = jnp.where(turn == i, aways[i], away)
        tile = lax.bitwise_xor(place[0], away)
        q_start = (tile * 2 + place[1]) * rows
        q_end = q_start + rows
        first, before, within = jnp.int32(0), jnp.int32(0), jnp.int32(0)
        for d in range(docs):
            begin = begins[d]
            first = jnp.where(begin <= q_start, begin, first)
            before = before + (begin <= q_start).astype(jnp.int32)
            within = within + (begin < q_end).astype(jnp.int32)
        q_pos = q_start + lax.broadcasted_iota(jnp.int32, (rows, 1), 0)

        def later_doc(d, firsts):
            begin = begins[d]
            return jnp.where(q_pos >= begin, begin, firsts)

        firsts = lax.fori_loop(before, within, later_doc, jnp.full((rows, 1), first, jnp.int32))
        needed = q_end - first
        q_at = pl.multiple_of(tile * (heads * rows), rows)

        def masked_scores(k_start, width):
            q = q_rows[pl.ds(q_at, heads * rows), :]
            k = kv_rows[0, pl.ds(k_start, width), :]
            s = lax.dot_general(q, k, (((1,), (1,)), ((), ())), preferred_element_type=jnp.float32)
            k_pos = k_start + lax.broadcasted_iota(jnp.int32, (rows, width), 1)
            allowed = (k_pos <= q_pos) & (k_pos >= firsts)
            s = jnp.where(allowed[None], s.reshape(heads, rows, width), far_below)
            return s.reshape(heads * rows, width)

        def put(value):
            for i, out in enumerate(outs):

                @pl.when(turn == i)
                def _(out=out):
                    out[...] = value.astype(jnp.bfloat16).reshape(out.shape)

        for lower, width in ((0, chunk // 2), (chunk // 2, chunk)):

            @pl.when((needed > lower) & (needed <= width))
            def _(width=width):
                k_start = pl.multiple_of(jnp.maximum(q_end - width, 0), rows)
                s = masked_scores(k_start, width)
                peak = jnp.max(s, axis=1, keepdims=True) * factor
                weights = jnp.exp2(s * factor - peak)
                sums = jnp.sum(weights, axis=1, keepdims=True)
                v = kv_rows[1, pl.ds(k_start, width), :]
                mixed[...] = jnp.dot(
                    weights.astype(jnp.bfloat16), v, preferred_element_type=jnp.float32
                ) * (1.0 / sums)

        @pl.when(needed > chunk)
        def _():
            chunks = lax.div(needed + chunk - 1, chunk)
            start = jnp.maximum(q_end - chunks * chunk, 0)
            top[...] = jnp.full_like(top, far_below)

            def score_chunk(j, carry):
                s = masked_scores(pl.multiple_of(start + j * chunk, rows), chunk)
                scores[j] = s
                top[...] = jnp.maximum(top[...], fold(s, jnp.maximum))
                return carry

            lax.fori_loop(0, chunks, score_chunk, 0)
            top[...] = jnp.broadcast_to(jnp.max(top[...], axis=1, keepdims=True) * factor, top.shape)
            total[...] = jnp.zeros_like(total)
            mixed[...] = jnp.zeros_like(mixed)

            def mix_chunk(j, carry):
                v = kv_rows[1, pl.ds(pl.multiple_of(start + j * chunk, rows), chunk), :]
                shift = jnp.concatenate([top[...]] * (chunk // 128), axis=1)
                weights = jnp.exp2(scores[j] * factor - shift)
                total[...] += fold(weights, jnp.add)
                mixed[...] += jnp.dot(
                    weights.astype(jnp.bfloat16), v, preferred_element_type=jnp.float32
                )
                return carry

            lax.fori_loop(0, chunks, mix_chunk, 0)
            mixed[...] = mixed[...] * (1.0 / jnp.sum(total[...], axis=1, keepdims=True))

        put(mixed[...])
        return carry

    lax.fori_loop(0, count, one_tile, 0)


def per_device(q_rows, k_rows, v_rows, doc_lengths, plan_dest, plan_slot):
    shards = lax.axis_size("seq")
    my_index = lax.axis_index("seq")
    rows, heads_all, head_size = q_rows.shape
    kv_heads = k_rows.shape[1]
    per = rows // shards
    span = rows * min(8, shards // 2)
    units = shards // 2
    unit, core = my_index // 2, my_index % 2
    heads = heads_all // units
    copies = units // kv_heads
    place = jnp.stack([unit, core]).astype(jnp.int32)

    q_send = q_rows.reshape(rows, units, heads, head_size).transpose(1, 2, 0, 3)
    kv_send = jnp.stack([k_rows, v_rows], axis=0).transpose(2, 0, 1, 3)
    kv_send = jnp.repeat(kv_send, copies, axis=0)
    sent = jnp.concatenate([q_send, kv_send], axis=1)

    def hop(x, distance):
        return lax.ppermute(x, "seq", [(i, i ^ distance) for i in range(shards)])

    def part(away):
        return lax.dynamic_index_in_dim(sent, unit ^ away, 0, keepdims=False)

    near = {away: part(away) for away in reversed(range(units))}
    for away in reversed(range(1, units)):
        near[away] = hop(near[away], 2 * away)
    half = units // 2
    far = {away: hop(near[away], 1) for away in range(units)}

    packed_shapes = (
        jax.ShapeDtypeStruct(((units + 1) * heads * shards, per, head_size), jnp.bfloat16),
        jax.ShapeDtypeStruct((2, shards * shards, per, head_size), jnp.bfloat16),
    )

    def pack(groups, arrays, packed, cost):
        blocks = [x.reshape(-1, per, head_size) for x in arrays]
        count = 2 + len(blocks)
        return pl.pallas_call(
            functools.partial(pack_kernel, groups=groups, heads=heads, shards=shards),
            out_shape=packed_shapes,
            in_specs=[smem] * 2 + [vmem] * (len(blocks) + len(packed)),
            out_specs=(vmem, vmem),
            input_output_aliases={count: 0, count + 1: 1} if packed else {},
            compiler_params=pltpu.CompilerParams(vmem_limit_bytes=24 << 20),
            cost_estimate=cost,
            name="pack_blocks",
        )(place, plan_dest * shards + plan_slot, *blocks, *packed)

    everyone = list(range(units))
    groups = [(column, away) for column in range(2) for away in everyone]
    packed = pack(groups, [x[away] for x in (near, far) for away in everyone], (), small)

    chunk = min(512, span)
    most = -(-(span + rows - 1) // chunk)
    tiles, raw = {}, {}

    def attend(aways, after):
        outs = pl.pallas_call(
            functools.partial(
                attend_kernel, aways=aways, heads=heads, shards=shards, rows=rows, chunk=chunk
            ),
            out_shape=[jax.ShapeDtypeStruct((heads, rows, head_size), jnp.bfloat16)] * len(aways),
            in_specs=[smem] * 2 + [vmem] * 2 + [anywhere] * len(after),
            out_specs=[vmem] * len(aways),
            scratch_shapes=[
                pltpu.SMEM((doc_lengths.shape[0],), jnp.int32),
                pltpu.VMEM((most, heads * rows, chunk), jnp.float32),
                pltpu.VMEM((heads * rows, 128), jnp.float32),
                pltpu.VMEM((heads * rows, 128), jnp.float32),
                pltpu.VMEM((heads * rows, head_size), jnp.float32),
            ],
            compiler_params=pltpu.CompilerParams(vmem_limit_bytes=24 << 20),
            cost_estimate=small,
            name="attend",
        )(place, doc_lengths, *packed, *after)
        for away, out in zip(aways, outs):
            raw[away] = out
            tiles[away] = hop(out, 2 * away) if away else out

    far_tiles = [half, half + 1] + list(reversed(range(half + 2, units)))
    attend((far_tiles[0], 1), [])
    attend((far_tiles[1], 2), [raw[far_tiles[0]]])
    for i in range(2, half, 2):
        attend(tuple(far_tiles[i : i + 2]), [tiles[1]])
    for away in range(3, half):
        attend((away,), [tiles[far_tiles[0]]])
    attend((0,), [tiles[far_tiles[1]]])
    gathered = jnp.zeros((units, heads, rows, head_size), jnp.bfloat16)
    for away in range(units):
        gathered = lax.dynamic_update_index_in_dim(gathered, tiles[away], unit ^ away, 0)
    return gathered.reshape(heads_all, rows, head_size).transpose(1, 0, 2)


def solution(mesh):
    whole = P(("dp", "seq"), None, None)
    return jax.shard_map(
        per_device,
        mesh=mesh,
        in_specs=(whole, whole, whole, P("dp"), P("dp"), P("dp")),
        out_specs=whole,
        check_vma=False,
    )
```
